256 devices in a mesh: teach: 4 (over x), vocab: 64 (over z, y, core), tok: 1.
Axes of the slice: x: 4, y: 4, z: 8, core: 2. Of those that a mesh axis runs over, the one named last changes fastest.
Arguments:
- teacher_logits: bfloat16 [4, 2048, 128256], P('teach', 'tok', 'vocab'), may hold values from -300 to 300
- teacher_weight: float32 [4], P('teach'), may hold values from 0.5 to 4
- student_logits: bfloat16 [2048, 128256], P(('tok', 'teach'), 'vocab'), may hold values from -300 to 300
Outputs:
- divergence: float32 [2048], P(('tok', 'teach'))
The draws below stay inside these ranges and needn't reach their ends.
All inputs are finite; a program needn't handle non-finite values.
Results may differ from the reference program's by a relative error of at most 0.0035.
Values may be sent and summed in bfloat16 or wider, within the bound.
A program may use at most 64 MiB of HBM per device.

```python
import math
import jax
import jax.numpy as jnp
from jax import lax

VOCAB = 128256
TOKENS = 2048
TEACHERS = 4


def shared_part(key):
    common_key = jax.random.fold_in(key, 41)
    return jnp.clip(jax.random.normal(common_key, (TOKENS, VOCAB), jnp.float32), -4.0, 4.0)


def row_scales(key, lead):
    low, high = (0.4, 4.0)
    return jnp.exp(jax.random.uniform(key, lead + (TOKENS, 1), jnp.float32, jnp.log(low), jnp.log(high)))


def linked_logits(base_key, key, lead):
    own_key, row_key = jax.random.split(key)
    own = jnp.clip(jax.random.normal(own_key, lead + (TOKENS, VOCAB), jnp.float32), -4.0, 4.0)
    return row_scales(row_key, lead) * (shared_part(base_key) + 0.7 * own)


def draw_teacher_logits(key, part):
    noise_key = jax.random.fold_in(jax.random.fold_in(key, 11), 0)
    base = linked_logits(key, noise_key, (TEACHERS,))
    values = base
    return values.astype(jnp.bfloat16)


def draw_student_logits(key, part):
    noise_key = jax.random.fold_in(jax.random.fold_in(key, 23), 0)
    base = linked_logits(key, noise_key, ())
    values = base
    return values.astype(jnp.bfloat16)


def steps_of(stream_key, shape, cuts, low, top_value):
    gain, own = 1.0, jax.random.fold_in(stream_key, 6)
    for dim, shards_of in cuts:
        steps = jnp.exp(jax.random.uniform(jax.random.fold_in(own, dim), (shards_of,), jnp.float32, low / len(cuts), top_value / len(cuts)))
        gain = gain * jnp.repeat(steps, shape[dim] // shards_of).reshape([-1 if axis == dim else 1 for axis in range(len(shape))])
    return gain


def setup_inputs(seed: int = 0, part: int = 0) -> dict:
    splits = jax.random.split(jax.random.key(seed), 4)
    own_keys = jax.random.split(jax.random.fold_in(splits[3], part), 4)
    return {
        "teacher_logits": draw_teacher_logits(jax.random.fold_in(jax.random.fold_in(splits[3], part), 71), part),
        "teacher_weight": jnp.clip(jnp.exp(math.log(4.0) - 2.0794415 * jax.random.uniform(splits[1], (TEACHERS,), jnp.float32) ** steps_of(splits[1], (TEACHERS,), ((0, 4),), -0.2, 0.2)), 0.5, 4.0),
        "student_logits": draw_student_logits(jax.random.fold_in(jax.random.fold_in(splits[3], part), 71), part),
    }


def block_divergence(teacher_block, student_block, share):
    scores = teacher_block.astype(jnp.float32)
    peak = jnp.max(scores, axis=2, keepdims=True)
    powers = jnp.exp(scores - peak)
    total = jnp.sum(powers, axis=2, keepdims=True)
    term = share[:, None, None] * (powers / total)
    term = lax.optimization_barrier(term.astype(jnp.bfloat16)).astype(jnp.float32)
    mixture = jnp.sum(term, axis=0)
    student = student_block.astype(jnp.float32)
    student_peak = jnp.max(student, axis=1, keepdims=True)
    student_total = jnp.sum(jnp.exp(student - student_peak), axis=1, keepdims=True)
    logq = student - student_peak - jnp.log(student_total)
    safe = jnp.maximum(mixture, 1e-30)
    return jnp.sum(mixture * (jnp.log(safe) - logq), axis=1)


def reference(teacher_logits, teacher_weight, student_logits):
    share = teacher_weight / jnp.sum(teacher_weight)
    block_rows = min(TOKENS, 256)
    block_count = TOKENS // block_rows
    teacher_blocks = teacher_logits.reshape(TEACHERS, block_count, block_rows, VOCAB).transpose(1, 0, 2, 3)
    student_blocks = student_logits.reshape(block_count, block_rows, VOCAB)
    result = lax.map(lambda pair: block_divergence(pair[0], pair[1], share), (teacher_blocks, student_blocks))
    return result.reshape(TOKENS)
```

```python
import functools

import jax
import jax.numpy as jnp
from jax import lax
from jax.experimental import pallas as pl
from jax.experimental.pallas import tpu as pltpu
from jax.sharding import PartitionSpec as P

MESH = pl.DeviceIdType.MESH
LANES = 128
BLOCK = 48


def over_rows(start, stop, body, carry):
    full = (stop - start) // BLOCK

    def step(i, carry):
        return body(pl.multiple_of(start + i * BLOCK, 16), BLOCK, carry)

    carry = lax.fori_loop(0, full, step, carry)
    rest = start + full * BLOCK
    return body(rest, stop - rest, carry) if rest < stop else carry


def folded(values, combine):
    rows = values.shape[0]
    parts = [values[first : first + 8] for first in range(0, rows - rows % 8, 8)]
    total = functools.reduce(combine, parts) if parts else None
    return total, values[rows - rows % 8 :] if rows % 8 else None


def kernel(
    sizes,
    weight_ref,
    scores,
    student_in,
    out_ref,
    held,
    student,
    opposite,
    near,
    sent_sum,
    got_sum,
    own_pair,
    stats,
    stats_got,
    beside,
    weights,
    final_one,
    final_two,
    local_sem,
    raw_send,
    raw_recv,
    sum_send,
    sum_recv,
    stats_send,
    stats_recv,
    side_send,
    side_recv,
    weight_send,
    weight_recv,
    final_send,
    final_recv,
):
    vocab_rows, tokens, mine, cores, ys, zs = sizes
    half = mine // 2
    x, v = lax.axis_index("teach"), lax.axis_index("vocab")
    plane = ys * cores
    z, y, core = v // plane, lax.rem(v // cores, ys), lax.rem(v, cores)

    def at(z_, y_, core_):
        return {"vocab": (lax.rem(z_, zs) * ys + lax.rem(y_, ys)) * cores + lax.rem(core_, cores)}

    right, left = {"teach": lax.rem(x + 1, 4)}, {"teach": lax.rem(x + 3, 4)}
    sides = (right, left)
    core_peer = at(z, y, core + 1)
    y_peers = (at(z, y + 1, core), at(z, y + ys - 1, core))
    z_peers = (at(z + 1, y, core), at(z + zs - 1, y, core))
    greeted = (right, left, core_peer, *y_peers, *z_peers)

    barrier = pltpu.get_barrier_semaphore()
    for peer in greeted:
        pl.semaphore_signal(barrier, inc=1, device_id=peer, device_id_type=MESH)

    block_copies = []
    for block in range(4):
        columns = pl.ds(block * mine, mine)
        block_copies.append(
            pltpu.make_async_copy(scores.at[:, columns], held.at[:, columns], local_sem.at[block])
        )
    student_copy = pltpu.make_async_copy(student_in, student, local_sem.at[4])
    for copy in (*block_copies, student_copy):
        copy.start()

    pl.semaphore_wait(barrier, len(greeted))

    def remote(source, target, send, recv, peer):
        return pltpu.make_async_remote_copy(
            src_ref=source,
            dst_ref=target,
            send_sem=send,
            recv_sem=recv,
            device_id=peer,
            device_id_type=MESH,
        )

    far = lax.rem(x + 2, 4)
    two_hop_base = (far * mine + half, far * mine)
    next_base = (lax.rem(x + 1, 4) * mine + half, lax.rem(x + 3, 4) * mine)
    one_hop_base = (lax.rem(x + 1, 4) * mine, lax.rem(x + 3, 4) * mine + half)
    pieces = half // LANES

    weights[0] = jnp.full((1, LANES), weight_ref[0], jnp.float32)
    weight_copies = [
        remote(weights.at[0], weights.at[1 + side], weight_send.at[side], weight_recv.at[side], sides[side])
        for side in range(2)
    ]
    for copy in weight_copies:
        copy.start()

    def raw(kind, bases, buffer, piece, side):
        columns = pl.ds(pl.multiple_of(bases[side] + piece * LANES, LANES), LANES)
        slot = (2 * kind + side) * pieces + piece
        return remote(
            scores.at[:, columns],
            buffer.at[side, :, pl.ds(piece * LANES, LANES)],
            raw_send.at[slot],
            raw_recv.at[slot],
            sides[side],
        )

    opposite_copies = [[raw(0, two_hop_base, opposite, p, s) for s in range(2)] for p in range(pieces)]
    near_copies = [[raw(1, one_hop_base, near, p, s) for s in range(2)] for p in range(pieces)]
    for pair in opposite_copies:
        for copy in pair:
            copy.start()
    for pair in near_copies[:-1]:
        for copy in pair:
            copy.start()

    wide = 2 * LANES

    def local_stats(ref, first, count, at_column):
        def one(i, _):
            columns = pl.ds(pl.multiple_of(first + i * wide, LANES), wide)

            def peak_body(row, rows, acc):
                block = ref[pl.ds(row, rows), columns].astype(jnp.float32)
                whole, rest = folded(block, jnp.maximum)
                acc8, acc4 = acc
                if whole is not None:
                    acc8 = jnp.maximum(acc8, whole)
                if rest is not None:
                    acc4 = jnp.maximum(acc4, rest.max(axis=0, keepdims=True))
                return acc8, acc4

            low = jnp.finfo(jnp.float32).min
            acc8, acc4 = over_rows(
                0, vocab_rows, peak_body, (jnp.full((8, wide), low), jnp.full((1, wide), low))
            )
            peak = jnp.maximum(acc8.max(axis=0, keepdims=True), acc4)

            def total_body(row, rows, acc):
                block = jnp.exp(ref[pl.ds(row, rows), columns].astype(jnp.float32) - peak)
                whole, rest = folded(block, jnp.add)
                acc8, acc4 = acc
                if whole is not None:
                    acc8 = acc8 + whole
                if rest is not None:
                    acc4 = acc4 + rest.sum(axis=0, keepdims=True)
                return acc8, acc4

            acc8, acc4 = over_rows(
                0, vocab_rows, total_body, (jnp.zeros((8, wide)), jnp.zeros((1, wide)))
            )
            put = pl.ds(pl.multiple_of(at_column + i * wide, LANES), wide)
            stats[0:1, put] = peak
            stats[1:2, put] = acc8.sum(axis=0, keepdims=True) + acc4
            return 0

        lax.fori_loop(0, count // wide, one, 0)

    student_copy.wait()
    local_stats(student, 0, mine, tokens)
    for block in range(4):
        block_copies[block].wait()
        local_stats(held, block * mine, mine, block * mine)

    def joined(slots):
        peak = stats[0:1]
        for slot in slots:
            peak = jnp.maximum(peak, stats_got[slot, 0:1])
        total = stats[1:2] * jnp.exp(stats[0:1] - peak)
        for slot in slots:
            total = total + stats_got[slot, 1:2] * jnp.exp(stats_got[slot, 0:1] - peak)
        stats[0:1] = peak
        stats[1:2] = total

    def stats_copy(slot, peer, source):
        return remote(source, stats_got.at[slot], stats_send.at[slot], stats_recv.at[slot], peer)

    def round_of(copies):
        for copy in copies:
            copy.start()
        for copy in copies:
            copy.wait()

    round_of([stats_copy(0, core_peer, stats)])
    joined([0])
    round_of([stats_copy(1, y_peers[0], stats), stats_copy(2, y_peers[1], stats)])
    round_of([stats_copy(3, y_peers[0], stats_got.at[1])])
    joined([1, 2, 3])
    round_of([stats_copy(4, z_peers[0], stats), stats_copy(5, z_peers[1], stats)])
    round_of([stats_copy(6, z_peers[0], stats_got.at[4]), stats_copy(7, z_peers[1], stats_got.at[5])])
    round_of([stats_copy(8, z_peers[0], stats_got.at[6]), stats_copy(9, z_peers[1], stats_got.at[7])])
    round_of([stats_copy(10, z_peers[0], stats_got.at[8])])
    joined([4, 5, 6, 7, 8, 9, 10])

    for copy in weight_copies:
        copy.wait()
    relay = remote(weights.at[1], weights.at[3], weight_send.at[2], weight_recv.at[2], right)
    relay.start()
    relay.wait()
    whole_weight = (weights[0] + weights[2]) + (weights[1] + weights[3])
    share = jnp.broadcast_to((weights[0] / whole_weight)[:, 0:1], (1, tokens))

    beside[0, 0:1] = stats[0:1, 0:tokens]
    beside[0, 1:2] = share / stats[1:2, 0:tokens]
    side_copies = [
        remote(beside.at[0], beside.at[1 + side], side_send.at[side], side_recv.at[side], sides[side])
        for side in range(2)
    ]
    for copy in side_copies:
        copy.start()
    for copy in near_copies[-1]:
        copy.start()
    for copy in side_copies:
        copy.wait()

    def term(ref, rows, columns, who, base):
        where = pl.ds(base, LANES)
        peak, factor = beside[who, 0:1, where], beside[who, 1:2, where]
        return jnp.exp(ref[rows, columns].astype(jnp.float32) - peak) * factor

    sum_rows = sent_sum.shape[1]
    cuts = [0, sum_rows // 3, 2 * (sum_rows // 3), sum_rows]

    def sum_copies_of(piece, side):
        columns = pl.ds(piece * LANES, LANES)
        spans = [(0, sum_rows)] if piece < pieces - 1 else list(zip(cuts[:-1], cuts[1:]))
        result = []
        for i, (first, last) in enumerate(spans):
            rows = pl.ds(first, last - first)
            slot = (side * pieces + piece) * 3 + i
            result.append(
                remote(
                    sent_sum.at[side, rows, columns],
                    got_sum.at[side, rows, columns],
                    sum_send.at[slot],
                    sum_recv.at[slot],
                    sides[side],
                )
            )
        return list(zip(spans, result))

    sum_copies = [[sum_copies_of(p, s) for s in range(2)] for p in range(pieces)]
    tail = sum_rows - 16
    sent_sum[:, tail:sum_rows] = jnp.zeros((2, 16, half), jnp.bfloat16)

    for piece in range(pieces):
        for side in range(2):
            opposite_copies[piece][side].wait_recv()
            columns = pl.ds(piece * LANES, LANES)
            base = pl.multiple_of(next_base[side] + piece * LANES, LANES)
            for (first, last), copy in sum_copies[piece][side]:

                def body(row, rows, carry):
                    span = pl.ds(row, rows)
                    total = term(held, span, pl.ds(base, LANES), 0, base) + term(
                        opposite.at[side], span, columns, 1 + side, base
                    )
                    sent_sum[side, span, columns] = total.astype(jnp.bfloat16)
                    return carry

                over_rows(first, min(last, vocab_rows), body, 0)
                copy.start()

    for piece in range(pieces):
        for side in range(2):
            near_copies[piece][side].wait_recv()
            place = side * half + piece * LANES
            base = pl.multiple_of(x * mine + place, LANES)

            def body(row, rows, carry):
                span = pl.ds(row, rows)
                own_pair[span, pl.ds(place, LANES)] = term(held, span, pl.ds(base, LANES), 0, base) + term(
                    near.at[side], span, pl.ds(piece * LANES, LANES), 1 + side, base
                )
                return carry

            over_rows(0, vocab_rows, body, 0)

    student_total = jnp.log(stats[1:2, tokens : tokens + mine])
    for piece in range(pieces):
        for side in range(2):
            place = (1 - side) * half + piece * LANES
            here = pl.ds(place, LANES)
            student_peak = stats[0:1, tokens + place : tokens + place + LANES]
            log_total = student_total[:, place : place + LANES]
            acc = (jnp.zeros((8, LANES)), jnp.zeros((1, LANES)))
            for (first, last), copy in sum_copies[piece][side]:
                copy.wait_recv()

                def body(row, rows, acc):
                    span = pl.ds(row, rows)
                    got = got_sum[side, span, pl.ds(piece * LANES, LANES)].astype(jnp.float32)
                    mixture = own_pair[span, here] + got
                    logq = student[span, here].astype(jnp.float32) - student_peak - log_total
                    value = mixture * (jnp.log(jnp.maximum(mixture, 1e-30)) - logq)
                    whole, rest = folded(value, jnp.add)
                    acc8, acc4 = acc
                    if whole is not None:
                        acc8 = acc8 + whole
                    if rest is not None:
                        acc4 = acc4 + rest.sum(axis=0, keepdims=True)
                    return acc8, acc4

                acc = over_rows(first, min(last, vocab_rows), body, acc)
            final_one[0, :, here] = acc[0].sum(axis=0, keepdims=True) + acc[1]

    mine_in_plane = lax.rem(v, plane)
    first_round = [
        remote(
            final_one.at[0],
            final_one.at[d],
            final_send.at[d],
            final_recv.at[d],
            {"vocab": z * plane + lax.rem(mine_in_plane + d, plane)},
        )
        for d in range(1, plane)
    ]
    for copy in first_round:
        copy.start()
    for copy in first_round:
        copy.wait_recv()
    total = jnp.zeros((1, mine))
    for i in range(plane):
        total = total + final_one[lax.rem(mine_in_plane + plane - i, plane)]
    final_two[0] = total
    second_round = [
        remote(
            final_two.at[0],
            final_two.at[d],
            final_send.at[plane + d],
            final_recv.at[plane + d],
            {"vocab": lax.rem(v + d * plane, zs * plane)},
        )
        for d in range(1, zs)
    ]
    for copy in second_round:
        copy.start()
    for copy in second_round:
        copy.wait_recv()
    total = jnp.zeros((1, mine))
    for i in range(zs):
        total = total + final_two[lax.rem(z + zs - i, zs)]
    out_ref[...] = total

    for copy in (*first_round, *second_round):
        copy.wait_send()
    for piece in range(pieces):
        for side in range(2):
            opposite_copies[piece][side].wait_send()
            near_copies[piece][side].wait_send()
            for _, copy in sum_copies[piece][side]:
                copy.wait_send()


def solution(mesh):
    def local(teacher_logits, teacher_weight, student_logits):
        scores, student = teacher_logits[0].T, student_logits.T
        vocab_rows, tokens = scores.shape
        mine = student.shape[1]
        half = mine // 2
        pieces = half // LANES
        ys, cores = 4, 2
        zs = mesh.shape["vocab"] // (ys * cores)
        sum_rows = -(-vocab_rows // BLOCK) * BLOCK
        together = tokens + mine
        f32, bf16 = jnp.float32, jnp.bfloat16
        dma = pltpu.SemaphoreType.DMA
        out = pl.pallas_call(
            functools.partial(kernel, (vocab_rows, tokens, mine, cores, ys, zs)),
            out_shape=jax.ShapeDtypeStruct((1, mine), f32),
            in_specs=[
                pl.BlockSpec(memory_space=pltpu.SMEM),
                pl.BlockSpec(memory_space=pl.ANY),
                pl.BlockSpec(memory_space=pl.ANY),
            ],
            out_specs=pl.BlockSpec(memory_space=pltpu.VMEM),
            scratch_shapes=[
                pltpu.VMEM((vocab_rows, tokens), bf16),
                pltpu.VMEM((vocab_rows, mine), bf16),
                pltpu.VMEM((2, vocab_rows, half), bf16),
                pltpu.VMEM((2, vocab_rows, half), bf16),
                pltpu.VMEM((2, sum_rows, half), bf16),
                pltpu.VMEM((2, sum_rows, half), bf16),
                pltpu.VMEM((vocab_rows, mine), f32),
                pltpu.VMEM((2, together), f32),
                pltpu.VMEM((11, 2, together), f32),
                pltpu.VMEM((3, 2, tokens), f32),
                pltpu.VMEM((4, 1, LANES), f32),
                pltpu.VMEM((ys * cores, 1, mine), f32),
                pltpu.VMEM((zs, 1, mine), f32),
                dma((5,)),
                dma((4 * pieces,)),
                dma((4 * pieces,)),
                dma((6 * pieces,)),
                dma((6 * pieces,)),
                dma((11,)),
                dma((11,)),
                dma((2,)),
                dma((2,)),
                dma((3,)),
                dma((3,)),
                dma((ys * cores + zs,)),
                dma((ys * cores + zs,)),
            ],
            compiler_params=pltpu.CompilerParams(
                collective_id=0, has_side_effects=True, vmem_limit_bytes=48 * 1024 * 1024
            ),
        )(teacher_weight, scores, student)
        return out.reshape(mine)

    in_specs = (P("teach", "tok", "vocab"), P("teach"), P(("tok", "teach"), "vocab"))
    out_specs = P(("tok", "teach"))
    return jax.shard_map(local, mesh=mesh, in_specs=in_specs, out_specs=out_specs, check_vma=False)
```

```python
import functools

import jax
import jax.numpy as jnp
from jax import lax
from jax.experimental import pallas as pl
from jax.experimental.pallas import tpu as pltpu
from jax.sharding import PartitionSpec as P

MESH = pl.DeviceIdType.MESH
LANES = 128
BLOCK = 48
CUTS = (0, 20, 34, 39, 42)


def over_rows(start, stop, body, carry):
    full = (stop - start) // BLOCK

    def step(i, carry):
        return body(pl.multiple_of(start + i * BLOCK, 16), BLOCK, carry)

    carry = lax.fori_loop(0, full, step, carry)
    rest = start + full * BLOCK
    return body(rest, stop - rest, carry) if rest < stop else carry


def folded(values, combine):
    rows = values.shape[0]
    parts = [values[first : first + 8] for first in range(0, rows - rows % 8, 8)]
    total = functools.reduce(combine, parts) if parts else None
    return total, values[rows - rows % 8 :] if rows % 8 else None


def kernel(
    sizes,
    weight_in,
    scores,
    student_in,
    out_ref,
    weight,
    held,
    student,
    opposite,
    near,
    sent_sum,
    got_sum,
    own_pair,
    stats,
    stats_got,
    beside,
    weights,
    final,
    local_sem,
    raw_send,
    raw_recv,
    sum_send,
    sum_recv,
    stats_send,
    stats_recv,
    side_send,
    side_recv,
    weight_send,
    weight_recv,
    final_send,
    final_recv,
    known_sem,
):
    vocab_rows, tokens, mine, cores, ys, zs = sizes
    half = mine // 2
    x, v = lax.axis_index("teach"), lax.axis_index("vocab")
    plane = ys * cores
    z, y, core = v // plane, lax.rem(v // cores, ys), lax.rem(v, cores)

    def at(z_, y_, core_):
        return {"vocab": (lax.rem(z_, zs) * ys + lax.rem(y_, ys)) * cores + lax.rem(core_, cores)}

    right, left = {"teach": lax.rem(x + 1, 4)}, {"teach": lax.rem(x + 3, 4)}
    sides = (right, left)
    core_peer = at(z, y, core + 1)
    y_peers = (at(z, y + 1, core), at(z, y + ys - 1, core))
    z_peers = (at(z + 1, y, core), at(z + zs - 1, y, core))
    greeted = (right, left, core_peer, *y_peers, *z_peers)

    barrier = pltpu.get_barrier_semaphore()
    for peer in greeted:
        pl.semaphore_signal(barrier, inc=1, device_id=peer, device_id_type=MESH)

    block_copies = []
    for block in range(4):
        columns = pl.ds(block * mine, mine)
        block_copies.append(
            pltpu.make_async_copy(scores.at[:, columns], held.at[:, columns], local_sem.at[block])
        )
    student_copy = pltpu.make_async_copy(student_in, student, local_sem.at[4])
    weight_copy = pltpu.make_async_copy(weight_in, weight, local_sem.at[5])
    for copy in (weight_copy, student_copy, *block_copies):
        copy.start()
    weight_copy.wait()
    weights[0] = jnp.full((1, LANES), weight[0], jnp.float32)

    pl.semaphore_wait(barrier, len(greeted))

    def remote(source, target, send, recv, peer):
        return pltpu.make_async_remote_copy(
            src_ref=source,
            dst_ref=target,
            send_sem=send,
            recv_sem=recv,
            device_id=peer,
            device_id_type=MESH,
        )

    far = lax.rem(x + 2, 4)
    two_hop_base = (far * mine + half, far * mine)
    next_base = (lax.rem(x + 1, 4) * mine + half, lax.rem(x + 3, 4) * mine)
    one_hop_base = (lax.rem(x + 1, 4) * mine, lax.rem(x + 3, 4) * mine + half)
    pieces = half // LANES

    weight_copies = [
        remote(weights.at[0], weights.at[1 + side], weight_send.at[side], weight_recv.at[side], sides[side])
        for side in range(2)
    ]
    for copy in weight_copies:
        copy.start()

    def raw(kind, bases, buffer, piece, side):
        columns = pl.ds(pl.multiple_of(bases[side] + piece * LANES, LANES), LANES)
        slot = (2 * kind + side) * pieces + piece
        return remote(
            scores.at[:, columns],
            buffer.at[side, :, pl.ds(piece * LANES, LANES)],
            raw_send.at[slot],
            raw_recv.at[slot],
            sides[side],
        )

    opposite_copies = [[raw(0, two_hop_base, opposite, p, s) for s in range(2)] for p in range(pieces)]
    near_copies = [[raw(1, one_hop_base, near, p, s) for s in range(2)] for p in range(pieces)]
    for pair in opposite_copies:
        for copy in pair:
            copy.start()
    for pair in near_copies[:-1]:
        for copy in pair:
            copy.start()

    def known(stage, peers):
        for peer in peers:
            pl.semaphore_signal(known_sem.at[stage], inc=1, device_id=peer, device_id_type=MESH)

    known(0, (core_peer, *y_peers, *z_peers))

    wide = 2 * LANES

    def local_stats(ref, first, count, at_column):
        def one(i, _):
            columns = pl.ds(pl.multiple_of(first + i * wide, LANES), wide)

            def peak_body(row, rows, acc):
                block = ref[pl.ds(row, rows), columns].astype(jnp.float32)
                whole, rest = folded(block, jnp.maximum)
                acc8, acc4 = acc
                if whole is not None:
                    acc8 = jnp.maximum(acc8, whole)
                if rest is not None:
                    acc4 = jnp.maximum(acc4, rest.max(axis=0, keepdims=True))
                return acc8, acc4

            low = jnp.finfo(jnp.float32).min
            acc8, acc4 = over_rows(
                0, vocab_rows, peak_body, (jnp.full((8, wide), low), jnp.full((1, wide), low))
            )
            peak = jnp.maximum(acc8.max(axis=0, keepdims=True), acc4)

            def total_body(row, rows, acc):
                block = jnp.exp(ref[pl.ds(row, rows), columns].astype(jnp.float32) - peak)
                whole, rest = folded(block, jnp.add)
                acc8, acc4 = acc
                if whole is not None:
                    acc8 = acc8 + whole
                if rest is not None:
                    acc4 = acc4 + rest.sum(axis=0, keepdims=True)
                return acc8, acc4

            acc8, acc4 = over_rows(
                0, vocab_rows, total_body, (jnp.zeros((8, wide)), jnp.zeros((1, wide)))
            )
            put = pl.ds(pl.multiple_of(at_column + i * wide, LANES), wide)
            stats[0:1, put] = peak
            stats[1:2, put] = acc8.sum(axis=0, keepdims=True) + acc4
            return 0

        lax.fori_loop(0, count // wide, one, 0)

    student_copy.wait()
    local_stats(student, 0, mine, tokens)
    pl.semaphore_wait(known_sem.at[0], 5)
    known(1, (at(z + 2, y, core), at(z + zs - 2, y, core)))
    for block in range(4):
        block_copies[block].wait()
        local_stats(held, block * mine, mine, block * mine)

    def joined(slots):
        peak = stats[0:1]
        for slot in slots:
            peak = jnp.maximum(peak, stats_got[slot, 0:1])
        total = stats[1:2] * jnp.exp(stats[0:1] - peak)
        for slot in slots:
            total = total + stats_got[slot, 1:2] * jnp.exp(stats_got[slot, 0:1] - peak)
        stats[0:1] = peak
        stats[1:2] = total

    def stats_copy(slot, peer, source):
        return remote(source, stats_got.at[slot], stats_send.at[slot], stats_recv.at[slot], peer)

    def round_of(copies):
        for copy in copies:
            copy.start()
        for copy in copies:
            copy.wait()

    round_of([stats_copy(0, core_peer, stats)])
    joined([0])
    round_of([stats_copy(d, at(z, y + d, core), stats) for d in (2, 1, 3)])
    joined([1, 2, 3])
    pl.semaphore_wait(known_sem.at[1], 2)
    round_of([stats_copy(3 + d, at(z + d, y, core), stats) for d in (4, 3, 5, 2, 6, 1, 7)])
    joined(range(4, 11))

    for copy in weight_copies:
        copy.wait()
    relay = remote(weights.at[1], weights.at[3], weight_send.at[2], weight_recv.at[2], right)
    relay.start()
    relay.wait()
    whole_weight = (weights[0] + weights[2]) + (weights[1] + weights[3])
    share = jnp.broadcast_to((weights[0] / whole_weight)[:, 0:1], (1, tokens))

    beside[0, 0:1] = stats[0:1, 0:tokens]
    beside[0, 1:2] = share / stats[1:2, 0:tokens]
    side_copies = [
        remote(beside.at[0], beside.at[1 + side], side_send.at[side], side_recv.at[side], sides[side])
        for side in range(2)
    ]
    for copy in side_copies:
        copy.start()
    for copy in near_copies[-1]:
        copy.start()
    for copy in side_copies:
        copy.wait()

    def term(ref, rows, columns, who, base):
        where = pl.ds(base, LANES)
        peak, factor = beside[who, 0:1, where], beside[who, 1:2, where]
        return jnp.exp(ref[rows, columns].astype(jnp.float32) - peak) * factor

    sum_rows = sent_sum.shape[1]
    cuts = [cut * (sum_rows // CUTS[-1]) for cut in CUTS]

    def sum_copies_of(piece, side):
        columns = pl.ds(piece * LANES, LANES)
        spans = [(0, sum_rows)] if piece < pieces - 1 else list(zip(cuts[:-1], cuts[1:]))
        result = []
        for i, (first, last) in enumerate(spans):
            rows = pl.ds(first, last - first)
            slot = (side * pieces + piece) * (len(cuts) - 1) + i
            result.append(
                remote(
                    sent_sum.at[side, rows, columns],
                    got_sum.at[side, rows, columns],
                    sum_send.at[slot],
                    sum_recv.at[slot],
                    sides[side],
                )
            )
        return list(zip(spans, result))

    sum_copies = [[sum_copies_of(p, s) for s in range(2)] for p in range(pieces)]
    tail = sum_rows - 16
    sent_sum[:, tail:sum_rows] = jnp.zeros((2, 16, half), jnp.bfloat16)

    for piece in range(pieces):
        for side in range(2):
            opposite_copies[piece][side].wait_recv()
            columns = pl.ds(piece * LANES, LANES)
            base = pl.multiple_of(next_base[side] + piece * LANES, LANES)
            for (first, last), copy in sum_copies[piece][side]:

                def body(row, rows, carry):
                    span = pl.ds(row, rows)
                    total = term(held, span, pl.ds(base, LANES), 0, base) + term(
                        opposite.at[side], span, columns, 1 + side, base
                    )
                    sent_sum[side, span, columns] = total.astype(jnp.bfloat16)
                    return carry

                over_rows(first, min(last, vocab_rows), body, 0)
                copy.start()

    for piece in range(pieces):
        for side in range(2):
            near_copies[piece][side].wait_recv()
            place = side * half + piece * LANES
            base = pl.multiple_of(x * mine + place, LANES)

            def body(row, rows, carry):
                span = pl.ds(row, rows)
                own_pair[span, pl.ds(place, LANES)] = term(held, span, pl.ds(base, LANES), 0, base) + term(
                    near.at[side], span, pl.ds(piece * LANES, LANES), 1 + side, base
                )
                return carry

            over_rows(0, vocab_rows, body, 0)

    def hops(d):
        dz, dy = d // plane, d // cores % ys
        return min(dz, zs - dz) + min(dy, ys - dy)

    others = sorted(range(1, zs * plane), key=lambda d: -hops(d))

    def spread(piece):
        for d in others:
            dz, dy, dc = d // plane, d // cores % ys, d % cores
            remote(
                final.at[piece, v],
                final.at[piece, v],
                final_send.at[piece],
                final_recv.at[piece],
                at(z + dz, y + dy, core + dc),
            ).start()

    def spread_done(piece):
        every = final.at[piece, pl.ds(0, len(others))]
        return pltpu.make_async_copy(every, every, final_recv.at[piece]), pltpu.make_async_copy(
            every, every, final_send.at[piece]
        )

    student_total = jnp.log(stats[1:2, tokens : tokens + mine])

    def divergence_part(piece, side, first, last, acc):
        place = (1 - side) * half + piece * LANES
        here = pl.ds(place, LANES)
        student_peak = stats[0:1, tokens + place : tokens + place + LANES]
        log_total = student_total[:, place : place + LANES]

        def body(row, rows, acc):
            span = pl.ds(row, rows)
            got = got_sum[side, span, pl.ds(piece * LANES, LANES)].astype(jnp.float32)
            mixture = own_pair[span, here] + got
            logq = student[span, here].astype(jnp.float32) - student_peak - log_total
            value = mixture * (jnp.log(jnp.maximum(mixture, 1e-30)) - logq)
            whole, rest = folded(value, jnp.add)
            acc8, acc4 = acc
            if whole is not None:
                acc8 = acc8 + whole
            if rest is not None:
                acc4 = acc4 + rest.sum(axis=0, keepdims=True)
            return acc8, acc4

        return over_rows(first, min(last, vocab_rows), body, acc)

    for piece in range(pieces):
        accs = [(jnp.zeros((8, LANES)), jnp.zeros((1, LANES)))] * 2
        for both in zip(*sum_copies[piece]):
            for side, ((first, last), copy) in enumerate(both):
                copy.wait_recv()
                accs[side] = divergence_part(piece, side, first, last, accs[side])
        for side in range(2):
            part = accs[side][0].sum(axis=0, keepdims=True) + accs[side][1]
            final[piece, v, :, (1 - side) * LANES : (2 - side) * LANES] = part
        spread(piece)
    for piece in range(pieces):
        spread_done(piece)[0].wait()
        total = final[piece].sum(axis=0)
        for part in range(2):
            place = part * half + piece * LANES
            out_ref[:, place : place + LANES] = total[:, part * LANES : (part + 1) * LANES]

    for piece in range(pieces):
        spread_done(piece)[1].wait()
    for piece in range(pieces):
        for side in range(2):
            opposite_copies[piece][side].wait_send()
            near_copies[piece][side].wait_send()
            for _, copy in sum_copies[piece][side]:
                copy.wait_send()


def solution(mesh):
    def local(teacher_logits, teacher_weight, student_logits):
        scores, student = teacher_logits[0].T, student_logits.T
        vocab_rows, tokens = scores.shape
        mine = student.shape[1]
        half = mine // 2
        pieces = half // LANES
        ys, cores = 4, 2
        everyone = mesh.shape["vocab"]
        zs = everyone // (ys * cores)
        sum_rows = -(-vocab_rows // BLOCK) * BLOCK
        together = tokens + mine
        f32, bf16 = jnp.float32, jnp.bfloat16
        dma = pltpu.SemaphoreType.DMA
        out = pl.pallas_call(
            functools.partial(kernel, (vocab_rows, tokens, mine, cores, ys, zs)),
            out_shape=jax.ShapeDtypeStruct((1, mine), f32),
            in_specs=[
                pl.BlockSpec(memory_space=pl.ANY),
                pl.BlockSpec(memory_space=pl.ANY),
                pl.BlockSpec(memory_space=pl.ANY),
            ],
            out_specs=pl.BlockSpec(memory_space=pltpu.VMEM),
            scratch_shapes=[
                pltpu.SMEM((1,), f32),
                pltpu.VMEM((vocab_rows, tokens), bf16),
                pltpu.VMEM((vocab_rows, mine), bf16),
                pltpu.VMEM((2, vocab_rows, half), bf16),
                pltpu.VMEM((2, vocab_rows, half), bf16),
                pltpu.VMEM((2, sum_rows, half), bf16),
                pltpu.VMEM((2, sum_rows, half), bf16),
                pltpu.VMEM((vocab_rows, mine), f32),
                pltpu.VMEM((2, together), f32),
                pltpu.VMEM((11, 2, together), f32),
                pltpu.VMEM((3, 2, tokens), f32),
                pltpu.VMEM((4, 1, LANES), f32),
                pltpu.VMEM((pieces, everyone, 1, 2 * LANES), f32),
                dma((6,)),
                dma((4 * pieces,)),
                dma((4 * pieces,)),
                dma((2 * pieces * (len(CUTS) - 1),)),
                dma((2 * pieces * (len(CUTS) - 1),)),
                dma((11,)),
                dma((11,)),
                dma((2,)),
                dma((2,)),
                dma((3,)),
                dma((3,)),
                dma((pieces,)),
                dma((pieces,)),
                pltpu.SemaphoreType.REGULAR((2,)),
            ],
            compiler_params=pltpu.CompilerParams(
                collective_id=0, has_side_effects=True, vmem_limit_bytes=60 * 1024 * 1024
            ),
        )(teacher_weight, scores, student)
        return out.reshape(mine)

    in_specs = (P("teach", "tok", "vocab"), P("teach"), P(("tok", "teach"), "vocab"))
    out_specs = P(("tok", "teach"))
    return jax.shard_map(local, mesh=mesh, in_specs=in_specs, out_specs=out_specs, check_vma=False)
```

```python
import functools

import jax
import jax.numpy as jnp
from jax import lax
from jax.experimental import pallas as pl
from jax.experimental.pallas import tpu as pltpu
from jax.sharding import PartitionSpec as P

MESH = pl.DeviceIdType.MESH
LANES = 128
BLOCK = 240
CUT = 48
CUTS = (0, 20, 34, 39, 42)


def over_rows(start, stop, body, carry):
    full = (stop - start) // BLOCK

    def step(i, carry):
        return body(pl.multiple_of(start + i * BLOCK, 16), BLOCK, carry)

    carry = lax.fori_loop(0, full, step, carry)
    rest = start + full * BLOCK
    return body(rest, stop - rest, carry) if rest < stop else carry


def folded(values, combine, group=8):
    rows = values.shape[0]
    left = rows % group
    parts = [values[first : first + group] for first in range(0, rows - left, group)]
    total = functools.reduce(combine, parts) if parts else None
    return total, values[rows - left :] if left else None


def kernel(
    sizes,
    weight,
    scores,
    student_in,
    out_ref,
    held,
    student,
    opposite,
    near,
    sent_sum,
    got_sum,
    own_pair,
    stats,
    stats_got,
    beside,
    weights,
    final,
    local_sem,
    raw_send,
    raw_recv,
    sum_send,
    sum_recv,
    stats_send,
    stats_recv,
    side_send,
    side_recv,
    weight_send,
    weight_recv,
    final_send,
    final_recv,
    known_sem,
):
    vocab_rows, tokens, mine, cores, ys, zs = sizes
    half = mine // 2
    x, v = lax.axis_index("teach"), lax.axis_index("vocab")
    plane = ys * cores
    z, y, core = v // plane, lax.rem(v // cores, ys), lax.rem(v, cores)

    def at(z_, y_, core_):
        return {"vocab": (lax.rem(z_, zs) * ys + lax.rem(y_, ys)) * cores + lax.rem(core_, cores)}

    right, left = {"teach": lax.rem(x + 1, 4)}, {"teach": lax.rem(x + 3, 4)}
    sides = (right, left)
    core_peer = at(z, y, core + 1)
    y_peers = (at(z, y + 1, core), at(z, y + ys - 1, core))
    z_peers = (at(z + 1, y, core), at(z + zs - 1, y, core))
    greeted = (right, left, core_peer, *y_peers, *z_peers)

    barrier = pltpu.get_barrier_semaphore()
    for peer in greeted:
        pl.semaphore_signal(barrier, inc=1, device_id=peer, device_id_type=MESH)

    block_copies = []
    for block in range(4):
        columns = pl.ds(block * mine, mine)
        block_copies.append(
            pltpu.make_async_copy(scores.at[:, columns], held.at[:, columns], local_sem.at[block])
        )
    student_copy = pltpu.make_async_copy(student_in, student, local_sem.at[4])
    for copy in (student_copy, *block_copies):
        copy.start()
    weights[0] = jnp.full((1, LANES), weight[0], jnp.float32)

    pl.semaphore_wait(barrier, len(greeted))

    def remote(source, target, send, recv, peer):
        return pltpu.make_async_remote_copy(
            src_ref=source,
            dst_ref=target,
            send_sem=send,
            recv_sem=recv,
            device_id=peer,
            device_id_type=MESH,
        )

    far = lax.rem(x + 2, 4)
    two_hop_base = (far * mine + half, far * mine)
    next_base = (lax.rem(x + 1, 4) * mine + half, lax.rem(x + 3, 4) * mine)
    one_hop_base = (lax.rem(x + 1, 4) * mine, lax.rem(x + 3, 4) * mine + half)
    pieces = half // LANES

    weight_copies = [
        remote(weights.at[0], weights.at[1 + side], weight_send.at[side], weight_recv.at[side], sides[side])
        for side in range(2)
    ]
    for copy in weight_copies:
        copy.start()

    def raw(kind, bases, buffer, piece, side):
        columns = pl.ds(pl.multiple_of(bases[side] + piece * LANES, LANES), LANES)
        slot = (2 * kind + side) * pieces + piece
        return remote(
            scores.at[:, columns],
            buffer.at[side, :, pl.ds(piece * LANES, LANES)],
            raw_send.at[slot],
            raw_recv.at[slot],
            sides[side],
        )

    opposite_copies = [[raw(0, two_hop_base, opposite, p, s) for s in range(2)] for p in range(pieces)]
    near_copies = [[raw(1, one_hop_base, near, p, s) for s in range(2)] for p in range(pieces)]
    for pair in opposite_copies:
        for copy in pair:
            copy.start()
    for pair in near_copies[:-1]:
        for copy in pair:
            copy.start()

    def known(stage, peers):
        for peer in peers:
            pl.semaphore_signal(known_sem.at[stage], inc=1, device_id=peer, device_id_type=MESH)

    known(0, (core_peer, *y_peers, *z_peers))

    wide = 2 * LANES

    def local_stats(ref, first, count, at_column):
        def one(i, _):
            columns = pl.ds(pl.multiple_of(first + i * wide, LANES), wide)

            def peak_body(row, rows, acc):
                whole, rest = folded(ref[pl.ds(row, rows), columns], jnp.maximum, 16)
                acc8, acc4 = acc
                if whole is not None:
                    acc8 = jnp.maximum(acc8, whole)
                if rest is not None:
                    acc4 = jnp.maximum(acc4, rest.astype(jnp.float32).max(axis=0, keepdims=True))
                return acc8, acc4

            low = -1e30
            acc8, acc4 = over_rows(
                0, vocab_rows, peak_body, (jnp.full((16, wide), low, ref.dtype), jnp.full((1, wide), low))
            )
            peak = jnp.maximum(acc8.astype(jnp.float32).max(axis=0, keepdims=True), acc4)

            def total_body(row, rows, acc):
                block = jnp.exp(ref[pl.ds(row, rows), columns].astype(jnp.float32) - peak)
                whole, rest = folded(block, jnp.add)
                acc8, acc4 = acc
                if whole is not None:
                    acc8 = acc8 + whole
                if rest is not None:
                    acc4 = acc4 + rest.sum(axis=0, keepdims=True)
                return acc8, acc4

            acc8, acc4 = over_rows(
                0, vocab_rows, total_body, (jnp.zeros((8, wide)), jnp.zeros((1, wide)))
            )
            put = pl.ds(pl.multiple_of(at_column + i * wide, LANES), wide)
            stats[0:1, put] = peak
            stats[1:2, put] = acc8.sum(axis=0, keepdims=True) + acc4
            return 0

        lax.fori_loop(0, count // wide, one, 0)

    student_copy.wait()
    local_stats(student, 0, mine, tokens)
    pl.semaphore_wait(known_sem.at[0], 5)
    known(1, (at(z + 2, y, core), at(z + zs - 2, y, core)))
    for block in range(4):
        block_copies[block].wait()
        local_stats(held, block * mine, mine, block * mine)

    def joined(slots):
        peak = stats[0:1]
        for slot in slots:
            peak = jnp.maximum(peak, stats_got[slot, 0:1])
        total = stats[1:2] * jnp.exp(stats[0:1] - peak)
        for slot in slots:
            total = total + stats_got[slot, 1:2] * jnp.exp(stats_got[slot, 0:1] - peak)
        stats[0:1] = peak
        stats[1:2] = total

    def stats_copy(slot, peer, source):
        return remote(source, stats_got.at[slot], stats_send.at[slot], stats_recv.at[slot], peer)

    def round_of(copies):
        for copy in copies:
            copy.start()
        for copy in copies:
            copy.wait()

    round_of([stats_copy(0, core_peer, stats)])
    joined([0])
    round_of([stats_copy(d, at(z, y + d, core), stats) for d in (2, 1, 3)])
    joined([1, 2, 3])
    pl.semaphore_wait(known_sem.at[1], 2)
    round_of([stats_copy(3 + d, at(z + d, y, core), stats) for d in (4, 3, 5, 2, 6, 1, 7)])
    joined(range(4, 11))

    for copy in weight_copies:
        copy.wait()
    relay = remote(weights.at[1], weights.at[3], weight_send.at[2], weight_recv.at[2], right)
    relay.start()
    relay.wait()
    whole_weight = (weights[0] + weights[2]) + (weights[1] + weights[3])
    share = jnp.broadcast_to((weights[0] / whole_weight)[:, 0:1], (1, tokens))

    beside[0, 0:1] = stats[0:1, 0:tokens]
    beside[0, 1:2] = share / stats[1:2, 0:tokens]
    side_copies = [
        remote(beside.at[0], beside.at[1 + side], side_send.at[side], side_recv.at[side], sides[side])
        for side in range(2)
    ]
    for copy in side_copies:
        copy.start()
    for copy in near_copies[-1]:
        copy.start()
    for copy in side_copies:
        copy.wait()

    def term(ref, rows, columns, who, base):
        where = pl.ds(base, LANES)
        peak, factor = beside[who, 0:1, where], beside[who, 1:2, where]
        return jnp.exp(ref[rows, columns].astype(jnp.float32) - peak) * factor

    sum_rows = sent_sum.shape[1]
    cuts = [cut * (sum_rows // CUTS[-1]) for cut in CUTS]

    def sum_copies_of(piece, side):
        columns = pl.ds(piece * LANES, LANES)
        spans = [(0, sum_rows)] if piece < pieces - 1 else list(zip(cuts[:-1], cuts[1:]))
        result = []
        for i, (first, last) in enumerate(spans):
            rows = pl.ds(first, last - first)
            slot = (side * pieces + piece) * (len(cuts) - 1) + i
            result.append(
                remote(
                    sent_sum.at[side, rows, columns],
                    got_sum.at[side, rows, columns],
                    sum_send.at[slot],
                    sum_recv.at[slot],
                    sides[side],
                )
            )
        return list(zip(spans, result))

    sum_copies = [[sum_copies_of(p, s) for s in range(2)] for p in range(pieces)]
    tail = sum_rows - 16
    sent_sum[:, tail:sum_rows] = jnp.zeros((2, 16, half), jnp.bfloat16)

    for piece in range(pieces):
        for side in range(2):
            opposite_copies[piece][side].wait_recv()
            columns = pl.ds(piece * LANES, LANES)
            base = pl.multiple_of(next_base[side] + piece * LANES, LANES)
            for (first, last), copy in sum_copies[piece][side]:

                def body(row, rows, carry):
                    span = pl.ds(row, rows)
                    total = term(held, span, pl.ds(base, LANES), 0, base) + term(
                        opposite.at[side], span, columns, 1 + side, base
                    )
                    sent_sum[side, span, columns] = total.astype(jnp.bfloat16)
                    return carry

                over_rows(first, min(last, vocab_rows), body, 0)
                copy.start()

    for piece in range(pieces):
        for side in range(2):
            near_copies[piece][side].wait_recv()
            place = side * half + piece * LANES
            base = pl.multiple_of(x * mine + place, LANES)

            def body(row, rows, carry):
                span = pl.ds(row, rows)
                own_pair[span, pl.ds(place, LANES)] = term(held, span, pl.ds(base, LANES), 0, base) + term(
                    near.at[side], span, pl.ds(piece * LANES, LANES), 1 + side, base
                )
                return carry

            over_rows(0, vocab_rows, body, 0)

    def hops(d):
        dz, dy = d // plane, d // cores % ys
        return min(dz, zs - dz) + min(dy, ys - dy)

    others = sorted(range(1, zs * plane), key=lambda d: -hops(d))

    def spread(piece):
        for d in others:
            dz, dy, dc = d // plane, d // cores % ys, d % cores
            remote(
                final.at[piece, v],
                final.at[piece, v],
                final_send.at[piece],
                final_recv.at[piece],
                at(z + dz, y + dy, core + dc),
            ).start()

    def spread_done(piece, semaphore):
        every = final.at[piece, pl.ds(0, len(others))]
        pltpu.make_async_copy(every, every, semaphore.at[piece]).wait()

    student_total = jnp.log(stats[1:2, tokens : tokens + mine])

    def divergence_part(piece, side, first, last, acc):
        place = (1 - side) * half + piece * LANES
        here = pl.ds(place, LANES)
        student_peak = stats[0:1, tokens + place : tokens + place + LANES]
        log_total = student_total[:, place : place + LANES]

        def body(row, rows, acc):
            span = pl.ds(row, rows)
            got = got_sum[side, span, pl.ds(piece * LANES, LANES)].astype(jnp.float32)
            mixture = own_pair[span, here] + got
            logq = student[span, here].astype(jnp.float32) - student_peak - log_total
            value = mixture * (jnp.log(jnp.maximum(mixture, 1e-30)) - logq)
            whole, rest = folded(value, jnp.add)
            acc8, acc4 = acc
            if whole is not None:
                acc8 = acc8 + whole
            if rest is not None:
                acc4 = acc4 + rest.sum(axis=0, keepdims=True)
            return acc8, acc4

        return over_rows(first, min(last, vocab_rows), body, acc)

    for piece in range(pieces):
        accs = [(jnp.zeros((8, LANES)), jnp.zeros((1, LANES)))] * 2
        for both in zip(*sum_copies[piece]):
            for side, ((first, last), copy) in enumerate(both):
                copy.wait_recv()
                accs[side] = divergence_part(piece, side, first, last, accs[side])
        for side in range(2):
            part = accs[side][0].sum(axis=0, keepdims=True) + accs[side][1]
            final[piece, v, :, (1 - side) * LANES : (2 - side) * LANES] = part
        spread(piece)
    for piece in range(pieces):
        spread_done(piece, final_recv)
        total = final[piece].sum(axis=0)
        for part in range(2):
            place = part * half + piece * LANES
            out_ref[:, place : place + LANES] = total[:, part * LANES : (part + 1) * LANES]

    for piece in range(pieces):
        spread_done(piece, final_send)
    for piece in range(pieces):
        for side in range(2):
            opposite_copies[piece][side].wait_send()
            near_copies[piece][side].wait_send()
            for _, copy in sum_copies[piece][side]:
                copy.wait_send()


def solution(mesh):
    def local(teacher_logits, teacher_weight, student_logits):
        scores, student = teacher_logits[0].T, student_logits.T
        vocab_rows, tokens = scores.shape
        mine = student.shape[1]
        half = mine // 2
        pieces = half // LANES
        ys, cores = 4, 2
        everyone = mesh.shape["vocab"]
        zs = everyone // (ys * cores)
        sum_rows = -(-vocab_rows // CUT) * CUT
        together = tokens + mine
        f32, bf16 = jnp.float32, jnp.bfloat16
        dma = pltpu.SemaphoreType.DMA
        out = pl.pallas_call(
            functools.partial(kernel, (vocab_rows, tokens, mine, cores, ys, zs)),
            out_shape=pltpu.VMEM((1, mine), f32),
            in_specs=[
                pl.BlockSpec(memory_space=pltpu.SMEM),
                pl.BlockSpec(memory_space=pltpu.HBM),
                pl.BlockSpec(memory_space=pltpu.HBM),
            ],
            out_specs=pl.BlockSpec(memory_space=pltpu.VMEM),
            scratch_shapes=[
                pltpu.VMEM((vocab_rows, tokens), bf16),
                pltpu.VMEM((vocab_rows, mine), bf16),
                pltpu.VMEM((2, vocab_rows, half), bf16),
                pltpu.VMEM((2, vocab_rows, half), bf16),
                pltpu.VMEM((2, sum_rows, half), bf16),
                pltpu.VMEM((2, sum_rows, half), bf16),
                pltpu.VMEM((vocab_rows, mine), f32),
                pltpu.VMEM((2, together), f32),
                pltpu.VMEM((11, 2, together), f32),
                pltpu.VMEM((3, 2, tokens), f32),
                pltpu.VMEM((4, 1, LANES), f32),
                pltpu.VMEM((pieces, everyone, 1, 2 * LANES), f32),
                dma((5,)),
                dma((4 * pieces,)),
                dma((4 * pieces,)),
                dma((2 * pieces * (len(CUTS) - 1),)),
                dma((2 * pieces * (len(CUTS) - 1),)),
                dma((11,)),
                dma((11,)),
                dma((2,)),
                dma((2,)),
                dma((3,)),
                dma((3,)),
                dma((pieces,)),
                dma((pieces,)),
                pltpu.SemaphoreType.REGULAR((2,)),
            ],
            compiler_params=pltpu.CompilerParams(
                collective_id=0, has_side_effects=True, vmem_limit_bytes=60 * 1024 * 1024
            ),
        )(teacher_weight, *(pltpu.with_memory_space_constraint(a, pltpu.HBM) for a in (scores, student)))
        return out.reshape(mine)

    in_specs = (P("teach", "tok", "vocab"), P("teach"), P(("tok", "teach"), "vocab"))
    out_specs = P(("tok", "teach"))
    return jax.shard_map(local, mesh=mesh, in_specs=in_specs, out_specs=out_specs, check_vma=False)
```

```python
import functools

import jax
import jax.numpy as jnp
from jax import lax
from jax.experimental import pallas as pl
from jax.experimental.pallas import tpu as pltpu
from jax.sharding import PartitionSpec as P

MESH = pl.DeviceIdType.MESH
LANES = 128
BLOCK = 240
CUTS = (0, 960, 1632, 1872)
GIVEN = 64


def over_rows(start, stop, body, carry):
    full = (stop - start) // BLOCK

    def step(i, carry):
        return body(pl.multiple_of(start + i * BLOCK, 16), BLOCK, carry)

    carry = lax.fori_loop(0, full, step, carry)
    rest = start + full * BLOCK
    return body(rest, stop - rest, carry) if rest < stop else carry


def folded(values, combine, group=8):
    rows = values.shape[0]
    left = rows % group
    parts = [values[first : first + group] for first in range(0, rows - left, group)]
    total = functools.reduce(combine, parts) if parts else None
    return total, values[rows - left :] if left else None


def kernel(
    sizes,
    weight,
    scores,
    student_in,
    out_ref,
    held,
    student,
    opposite,
    near,
    sent_sum,
    got_sum,
    own_pair,
    stats,
    stats_got,
    beside,
    weights,
    final,
    extra,
    extra_student,
    extra_opposite,
    extra_near,
    extra_sent,
    extra_got,
    extra_pair,
    local_sem,
    raw_send,
    raw_recv,
    sum_send,
    sum_recv,
    stats_send,
    stats_recv,
    side_send,
    side_recv,
    weight_send,
    weight_recv,
    final_send,
    final_recv,
    known_sem,
    give_send,
    give_recv,
    extra_send,
    extra_recv,
):
    vocab_rows, tokens, mine, cores, ys, zs = sizes
    half = mine // 2
    x, v = lax.axis_index("teach"), lax.axis_index("vocab")
    plane = ys * cores
    z, y, core = v // plane, lax.rem(v // cores, ys), lax.rem(v, cores)

    def at(z_, y_, core_):
        return {"vocab": (lax.rem(z_, zs) * ys + lax.rem(y_, ys)) * cores + lax.rem(core_, cores)}

    right, left = {"teach": lax.rem(x + 1, 4)}, {"teach": lax.rem(x + 3, 4)}
    sides = (right, left)
    core_peer = at(z, y, core + 1)
    y_peers = (at(z, y + 1, core), at(z, y + ys - 1, core))
    z_peers = (at(z + 1, y, core), at(z + zs - 1, y, core))
    takes = z < zs // 2 - 1
    gives = (z >= zs // 2) & (z < zs - 1)
    keeps = jnp.logical_not(gives)
    half_way = at(z + zs // 2, y, core)

    barrier = pltpu.get_barrier_semaphore()

    def greet(peer):
        pl.semaphore_signal(barrier, inc=1, device_id=peer, device_id_type=MESH)

    def along(place, size, next_peer, first_to_last, act):
        pl.when(place < size - 1)(lambda: act(next_peer))
        pl.when(place == 0)(lambda: act(first_to_last))

    def waited_for(place, size):
        return (place + size - 2) // (size - 1) + place // (size - 1)

    for peer in (right, left, core_peer):
        greet(peer)
    along(y, ys, y_peers[0], y_peers[1], greet)
    along(z, zs, z_peers[0], z_peers[1], greet)
    before = waited_for(y, ys) + waited_for(z, zs)

    block_copies = []
    for block in range(4):
        columns = pl.ds(block * mine, mine)
        block_copies.append(
            pltpu.make_async_copy(scores.at[:, columns], held.at[:, columns], local_sem.at[block])
        )
    student_copy = pltpu.make_async_copy(student_in, student, local_sem.at[4])
    for copy in (student_copy, *block_copies):
        copy.start()
    weights[0] = jnp.full((1, LANES), weight[0], jnp.float32)

    pl.semaphore_wait(barrier, 3 + before)

    def remote(source, target, send, recv, peer):
        return pltpu.make_async_remote_copy(
            src_ref=source,
            dst_ref=target,
            send_sem=send,
            recv_sem=recv,
            device_id=peer,
            device_id_type=MESH,
        )

    far = lax.rem(x + 2, 4)
    two_hop_base = (far * mine + half, far * mine)
    next_base = (lax.rem(x + 1, 4) * mine + half, lax.rem(x + 3, 4) * mine)
    one_hop_base = (lax.rem(x + 1, 4) * mine, lax.rem(x + 3, 4) * mine + half)
    pieces = half // LANES

    weight_copies = [
        remote(weights.at[0], weights.at[1 + side], weight_send.at[side], weight_recv.at[side], sides[side])
        for side in range(2)
    ]
    for copy in weight_copies:
        copy.start()

    class Either:
        def __init__(self, make, first, last):
            self.whole = make(first, last)
            self.less = make(GIVEN, last) if first < GIVEN else None

        def do(self, act):
            if self.less is None:
                act(self.whole)
            else:
                pl.when(keeps)(lambda: act(self.whole))
                pl.when(gives)(lambda: act(self.less))

        def start(self):
            self.do(lambda copy: copy.start())

        def wait_recv(self):
            self.do(lambda copy: copy.wait_recv())

        def wait_send(self):
            self.do(lambda copy: copy.wait_send())

    def raw(kind, bases, buffer, piece, side):
        columns = pl.ds(pl.multiple_of(bases[side] + piece * LANES, LANES), LANES)
        slot = (2 * kind + side) * pieces + piece

        def make(first, last):
            rows = pl.ds(first, last - first)
            return remote(
                scores.at[rows, columns],
                buffer.at[side, rows, pl.ds(piece * LANES, LANES)],
                raw_send.at[slot],
                raw_recv.at[slot],
                sides[side],
            )

        return Either(make, 0, vocab_rows)

    opposite_copies = [[raw(0, two_hop_base, opposite, p, s) for s in range(2)] for p in range(pieces)]
    near_copies = [[raw(1, one_hop_base, near, p, s) for s in range(2)] for p in range(pieces)]
    for pair in opposite_copies:
        for copy in pair:
            copy.start()
    for pair in near_copies[:-1]:
        for copy in pair:
            copy.start()

    def known(stage, peers):
        for peer in peers:
            pl.semaphore_signal(known_sem.at[stage], inc=1, device_id=peer, device_id_type=MESH)

    def answer(place, size, last_peer, last_to_first):
        pl.when(place > 0)(lambda: known(0, (last_peer,)))
        pl.when(place == size - 1)(lambda: known(0, (last_to_first,)))

    answer(y, ys, y_peers[1], y_peers[0])
    answer(z, zs, z_peers[1], z_peers[0])

    wide = 2 * LANES

    def local_stats(ref, first, count, at_column):
        def one(i, _):
            columns = pl.ds(pl.multiple_of(first + i * wide, LANES), wide)

            def peak_body(row, rows, acc):
                whole, rest = folded(ref[pl.ds(row, rows), columns], jnp.maximum, 16)
                acc8, acc4 = acc
                if whole is not None:
                    acc8 = jnp.maximum(acc8, whole)
                if rest is not None:
                    acc4 = jnp.maximum(acc4, rest.astype(jnp.float32).max(axis=0, keepdims=True))
                return acc8, acc4

            low = -1e30
            acc8, acc4 = over_rows(
                0, vocab_rows, peak_body, (jnp.full((16, wide), low, ref.dtype), jnp.full((1, wide), low))
            )
            peak = jnp.maximum(acc8.astype(jnp.float32).max(axis=0, keepdims=True), acc4)

            def total_body(row, rows, acc):
                block = jnp.exp(ref[pl.ds(row, rows), columns].astype(jnp.float32) - peak)
                whole, rest = folded(block, jnp.add)
                acc8, acc4 = acc
                if whole is not None:
                    acc8 = acc8 + whole
                if rest is not None:
                    acc4 = acc4 + rest.sum(axis=0, keepdims=True)
                return acc8, acc4

            acc8, acc4 = over_rows(
                0, vocab_rows, total_body, (jnp.zeros((8, wide)), jnp.zeros((1, wide)))
            )
            put = pl.ds(pl.multiple_of(at_column + i * wide, LANES), wide)
            stats[0:1, put] = peak
            stats[1:2, put] = acc8.sum(axis=0, keepdims=True) + acc4
            return 0

        lax.fori_loop(0, count // wide, one, 0)

    student_copy.wait()
    local_stats(student, 0, mine, tokens)
    pl.when(before < 4)(lambda: pl.semaphore_wait(known_sem.at[0], 4 - before))
    known(1, (*y_peers, *z_peers))
    for block in range(4):
        block_copies[block].wait()
        local_stats(held, block * mine, mine, block * mine)
        if block == 1:
            pl.semaphore_wait(known_sem.at[1], 4)
            known(2, (at(z + 2, y, core), at(z + zs - 2, y, core)))

    def joined(slots):
        peak = stats[0:1]
        for slot in slots:
            peak = jnp.maximum(peak, stats_got[slot, 0:1])
        total = stats[1:2] * jnp.exp(stats[0:1] - peak)
        for slot in slots:
            total = total + stats_got[slot, 1:2] * jnp.exp(stats_got[slot, 0:1] - peak)
        stats[0:1] = peak
        stats[1:2] = total

    def stats_copy(slot, peer, source):
        return remote(source, stats_got.at[slot], stats_send.at[slot], stats_recv.at[slot], peer)

    def round_of(copies):
        for copy in copies:
            copy.start()
        for copy in copies:
            copy.wait()

    round_of([stats_copy(0, core_peer, stats)])
    joined([0])
    round_of([stats_copy(d, at(z, y + d, core), stats) for d in (2, 1, 3)])
    joined([1, 2, 3])
    pl.semaphore_wait(known_sem.at[2], 2)
    round_of([stats_copy(3 + d, at(z + d, y, core), stats) for d in (4, 3, 5, 2, 6, 1, 7)])
    joined(range(4, 11))

    given_rows = pl.ds(0, GIVEN)
    give_copies = [
        remote(scores.at[given_rows], extra, give_send.at[0], give_recv.at[0], half_way),
        remote(student_in.at[given_rows], extra_student, give_send.at[1], give_recv.at[1], half_way),
    ]

    @pl.when(gives)
    def _():
        for copy in give_copies:
            copy.start()

    for copy in weight_copies:
        copy.wait()
    relay = remote(weights.at[1], weights.at[3], weight_send.at[2], weight_recv.at[2], right)
    relay.start()
    relay.wait()
    whole_weight = (weights[0] + weights[2]) + (weights[1] + weights[3])
    share = jnp.broadcast_to((weights[0] / whole_weight)[:, 0:1], (1, tokens))

    beside[0, 0:1] = stats[0:1, 0:tokens]
    beside[0, 1:2] = share / stats[1:2, 0:tokens]
    side_copies = [
        remote(beside.at[0], beside.at[1 + side], side_send.at[side], side_recv.at[side], sides[side])
        for side in range(2)
    ]
    for copy in side_copies:
        copy.start()
    for copy in near_copies[-1]:
        copy.start()
    for copy in side_copies:
        copy.wait()

    def term(ref, rows, columns, who, base, width=LANES):
        where = pl.ds(base, width)
        peak, factor = beside[who, 0:1, where], beside[who, 1:2, where]
        return jnp.exp(ref[rows, columns].astype(jnp.float32) - peak) * factor

    cuts = [*CUTS, vocab_rows]

    def sum_copies_of(piece, side):
        columns = pl.ds(piece * LANES, LANES)
        spans = [(0, vocab_rows)] if piece < pieces - 1 else list(zip(cuts[:-1], cuts[1:]))
        result = []
        for i, (first, last) in enumerate(spans):
            slot = (side * pieces + piece) * (len(cuts) - 1) + i

            def make(first, last):
                rows = pl.ds(first, last - first)
                return remote(
                    sent_sum.at[side, rows, columns],
                    got_sum.at[side, rows, columns],
                    sum_send.at[slot],
                    sum_recv.at[slot],
                    sides[side],
                )

            result.append(Either(make, first, last))
        return list(zip(spans, result))

    sum_copies = [[sum_copies_of(p, s) for s in range(2)] for p in range(pieces)]

    def extra_copy(kind, side, source, target):
        slot = 2 * kind + side
        return remote(source, target, extra_send.at[slot], extra_recv.at[slot], sides[side])

    def of_extra(bases, side):
        return extra.at[:, pl.ds(pl.multiple_of(bases[side], LANES), half)]

    extra_raw = [
        extra_copy(kind, side, of_extra(bases, side), buffer.at[side])
        for kind, (bases, buffer) in enumerate(((two_hop_base, extra_opposite), (one_hop_base, extra_near)))
        for side in range(2)
    ]
    extra_sums = [extra_copy(2, side, extra_sent.at[side], extra_got.at[side]) for side in range(2)]
    every = pl.ds(0, GIVEN)

    def send_extra_raw():
        for copy in give_copies:
            copy.wait_recv()
        for copy in extra_raw:
            copy.start()

    def send_extra_sums():
        for side in range(2):
            extra_raw[side].wait_recv()
            base = pl.multiple_of(next_base[side], LANES)
            total = term(extra, every, pl.ds(base, half), 0, base, half) + term(
                extra_opposite.at[side], every, pl.ds(0, half), 1 + side, base, half
            )
            extra_sent[side] = total.astype(jnp.bfloat16)
            extra_sums[side].start()

    def add_extra_pair():
        for side in range(2):
            extra_raw[2 + side].wait_recv()
            place = side * half
            base = pl.multiple_of(x * mine + place, LANES)
            extra_pair[:, place : place + half] = term(extra, every, pl.ds(base, half), 0, base, half) + term(
                extra_near.at[side], every, pl.ds(0, half), 1 + side, base, half
            )

    for piece in range(pieces):
        for side in range(2):
            opposite_copies[piece][side].wait_recv()
            columns = pl.ds(piece * LANES, LANES)
            base = pl.multiple_of(next_base[side] + piece * LANES, LANES)
            for (first, last), copy in sum_copies[piece][side]:

                def body(row, rows, carry):
                    span = pl.ds(row, rows)
                    total = term(held, span, pl.ds(base, LANES), 0, base) + term(
                        opposite.at[side], span, columns, 1 + side, base
                    )
                    sent_sum[side, span, columns] = total.astype(jnp.bfloat16)
                    return carry

                over_rows(first, last, body, 0)
                copy.start()
        pl.when(takes)(send_extra_raw if piece == 0 else send_extra_sums)

    for piece in range(pieces):
        for side in range(2):
            near_copies[piece][side].wait_recv()
            place = side * half + piece * LANES
            base = pl.multiple_of(x * mine + place, LANES)

            def body(row, rows, carry):
                span = pl.ds(row, rows)
                own_pair[span, pl.ds(place, LANES)] = term(held, span, pl.ds(base, LANES), 0, base) + term(
                    near.at[side], span, pl.ds(piece * LANES, LANES), 1 + side, base
                )
                return carry

            over_rows(0, vocab_rows, body, 0)
    pl.when(takes)(add_extra_pair)

    def hops(d):
        dz, dy = d // plane, d // cores % ys
        return min(dz, zs - dz) + min(dy, ys - dy)

    others = sorted(range(1, zs * plane), key=lambda d: -hops(d))

    def spread(piece):
        for d in others:
            dz, dy, dc = d // plane, d // cores % ys, d % cores
            remote(
                final.at[piece, v],
                final.at[piece, v],
                final_send.at[piece],
                final_recv.at[piece],
                at(z + dz, y + dy, core + dc),
            ).start()

    def spread_done(piece, semaphore):
        every = final.at[piece, pl.ds(0, len(others))]
        pltpu.make_async_copy(every, every, semaphore.at[piece]).wait()

    student_total = jnp.log(stats[1:2, tokens : tokens + mine])

    def divergences(pair, got, logits, place, width):
        mixture = pair + got.astype(jnp.float32)
        student_peak = stats[0:1, tokens + place : tokens + place + width]
        logq = logits.astype(jnp.float32) - student_peak - student_total[:, place : place + width]
        return mixture * (jnp.log(jnp.maximum(mixture, 1e-30)) - logq)

    def divergence_part(piece, side, first, last, acc):
        place = (1 - side) * half + piece * LANES
        here = pl.ds(place, LANES)

        def body(row, rows, acc):
            span = pl.ds(row, rows)
            got = got_sum[side, span, pl.ds(piece * LANES, LANES)]
            value = divergences(own_pair[span, here], got, student[span, here], place, LANES)
            whole, rest = folded(value, jnp.add)
            acc8, acc4 = acc
            if whole is not None:
                acc8 = acc8 + whole
            if rest is not None:
                acc4 = acc4 + rest.sum(axis=0, keepdims=True)
            return acc8, acc4

        return over_rows(first, last, body, acc)

    def add_extra_divergence():
        for side in range(2):
            extra_sums[side].wait_recv()
            place = (1 - side) * half
            here = pl.ds(place, half)
            value = divergences(extra_pair[:, here], extra_got[side], extra_student[:, here], place, half)
            part = value.sum(axis=0, keepdims=True)
            for piece in range(pieces):
                lanes = slice((1 - side) * LANES, (2 - side) * LANES)
                final[piece, v, :, lanes] = final[piece, v, :, lanes] + part[:, piece * LANES : (piece + 1) * LANES]

    for piece in range(pieces):
        accs = [(jnp.zeros((8, LANES)), jnp.zeros((1, LANES)))] * 2
        for both in zip(*sum_copies[piece]):
            for side, ((first, last), copy) in enumerate(both):
                copy.wait_recv()
                if first == 0:
                    head, rest = divergence_part(piece, side, 0, GIVEN, accs[side])
                    accs[side] = jnp.where(gives, 0.0, head), rest
                    first = GIVEN
                accs[side] = divergence_part(piece, side, first, last, accs[side])
        for side in range(2):
            part = accs[side][0].sum(axis=0, keepdims=True) + accs[side][1]
            final[piece, v, :, (1 - side) * LANES : (2 - side) * LANES] = part
        if piece < pieces - 1:
            pl.when(jnp.logical_not(takes))(functools.partial(spread, piece))

    @pl.when(takes)
    def _():
        add_extra_divergence()
        for piece in range(pieces - 1):
            spread(piece)

    spread(pieces - 1)
    for piece in range(pieces):
        spread_done(piece, final_recv)
        total = final[piece].sum(axis=0)
        for part in range(2):
            place = part * half + piece * LANES
            out_ref[:, place : place + LANES] = total[:, part * LANES : (part + 1) * LANES]

    for piece in range(pieces):
        spread_done(piece, final_send)
    for piece in range(pieces):
        for side in range(2):
            opposite_copies[piece][side].wait_send()
            near_copies[piece][side].wait_send()
            for _, copy in sum_copies[piece][side]:
                copy.wait_send()

    @pl.when(takes)
    def _():
        for copy in (*extra_raw, *extra_sums):
            copy.wait_send()

    @pl.when(gives)
    def _():
        for copy in give_copies:
            copy.wait_send()


def solution(mesh):
    def local(teacher_logits, teacher_weight, student_logits):
        scores, student = teacher_logits[0].T, student_logits.T
        vocab_rows, tokens = scores.shape
        mine = student.shape[1]
        half = mine // 2
        pieces = half // LANES
        ys, cores = 4, 2
        everyone = mesh.shape["vocab"]
        zs = everyone // (ys * cores)
        together = tokens + mine
        f32, bf16 = jnp.float32, jnp.bfloat16
        dma = pltpu.SemaphoreType.DMA
        out = pl.pallas_call(
            functools.partial(kernel, (vocab_rows, tokens, mine, cores, ys, zs)),
            out_shape=pltpu.VMEM((1, mine), f32),
            in_specs=[
                pl.BlockSpec(memory_space=pltpu.SMEM),
                pl.BlockSpec(memory_space=pltpu.HBM),
                pl.BlockSpec(memory_space=pltpu.HBM),
            ],
            out_specs=pl.BlockSpec(memory_space=pltpu.VMEM),
            scratch_shapes=[
                pltpu.VMEM((vocab_rows, tokens), bf16),
                pltpu.VMEM((vocab_rows, mine), bf16),
                pltpu.VMEM((2, vocab_rows, half), bf16),
                pltpu.VMEM((2, vocab_rows, half), bf16),
                pltpu.VMEM((2, vocab_rows, half), bf16),
                pltpu.VMEM((2, vocab_rows, half), bf16),
                pltpu.VMEM((vocab_rows, mine), f32),
                pltpu.VMEM((2, together), f32),
                pltpu.VMEM((11, 2, together), f32),
                pltpu.VMEM((3, 2, tokens), f32),
                pltpu.VMEM((4, 1, LANES), f32),
                pltpu.VMEM((pieces, everyone, 1, 2 * LANES), f32),
                pltpu.VMEM((GIVEN, tokens), bf16),
                pltpu.VMEM((GIVEN, mine), bf16),
                pltpu.VMEM((2, GIVEN, half), bf16),
                pltpu.VMEM((2, GIVEN, half), bf16),
                pltpu.VMEM((2, GIVEN, half), bf16),
                pltpu.VMEM((2, GIVEN, half), bf16),
                pltpu.VMEM((GIVEN, mine), f32),
                dma((5,)),
                dma((4 * pieces,)),
                dma((4 * pieces,)),
                dma((2 * pieces * len(CUTS),)),
                dma((2 * pieces * len(CUTS),)),
                dma((11,)),
                dma((11,)),
                dma((2,)),
                dma((2,)),
                dma((3,)),
                dma((3,)),
                dma((pieces,)),
                dma((pieces,)),
                pltpu.SemaphoreType.REGULAR((3,)),
                dma((2,)),
                dma((2,)),
                dma((6,)),
                dma((6,)),
            ],
            compiler_params=pltpu.CompilerParams(
                collective_id=0, has_side_effects=True, vmem_limit_bytes=60 * 1024 * 1024
            ),
        )(teacher_weight, *(pltpu.with_memory_space_constraint(a, pltpu.HBM) for a in (scores, student)))
        return out.reshape(mine)

    in_specs = (P("teach", "tok", "vocab"), P("teach"), P(("tok", "teach"), "vocab"))
    out_specs = P(("tok", "teach"))
    return jax.shard_map(local, mesh=mesh, in_specs=in_specs, out_specs=out_specs, check_vma=False)
```

```python
import functools

import jax
import jax.numpy as jnp
from jax import lax
from jax.experimental import pallas as pl
from jax.experimental.pallas import tpu as pltpu
from jax.sharding import PartitionSpec as P

MESH = pl.DeviceIdType.MESH
LANES = 128
BLOCK = 240
CUTS = (0, 960, 1632, 1872)
GIVEN = 64


def over_rows(start, stop, body, carry):
    full = (stop - start) // BLOCK

    def step(i, carry):
        return body(pl.multiple_of(start + i * BLOCK, 16), BLOCK, carry)

    carry = lax.fori_loop(0, full, step, carry)
    rest = start + full * BLOCK
    return body(rest, stop - rest, carry) if rest < stop else carry


def folded(values, combine, group=8):
    rows = values.shape[0]
    left = rows % group
    parts = [values[first : first + group] for first in range(0, rows - left, group)]
    total = functools.reduce(combine, parts) if parts else None
    return total, values[rows - left :] if left else None


def kernel(
    sizes,
    weight,
    scores,
    student_in,
    out_ref,
    held,
    student,
    opposite,
    near,
    sent_sum,
    got_sum,
    own_pair,
    stats,
    stats_got,
    beside,
    weights,
    final,
    extra,
    extra_student,
    extra_opposite,
    extra_near,
    extra_sent,
    extra_got,
    extra_pair,
    extra_part,
    local_sem,
    raw_send,
    raw_recv,
    sum_send,
    sum_recv,
    stats_send,
    stats_recv,
    side_send,
    side_recv,
    weight_send,
    weight_recv,
    final_send,
    final_recv,
    known_sem,
    give_send,
    give_recv,
    extra_send,
    extra_recv,
):
    vocab_rows, tokens, mine, cores, ys, zs = sizes
    half = mine // 2
    x, v = lax.axis_index("teach"), lax.axis_index("vocab")
    plane = ys * cores
    z, y, core = v // plane, lax.rem(v // cores, ys), lax.rem(v, cores)

    def at(z_, y_, core_):
        return {"vocab": (lax.rem(z_, zs) * ys + lax.rem(y_, ys)) * cores + lax.rem(core_, cores)}

    right, left = {"teach": lax.rem(x + 1, 4)}, {"teach": lax.rem(x + 3, 4)}
    sides = (right, left)
    core_peer = at(z, y, core + 1)
    y_peers = (at(z, y + 1, core), at(z, y + ys - 1, core))
    z_peers = (at(z + 1, y, core), at(z + zs - 1, y, core))
    takes = z < zs // 2 - 1
    gives = z >= zs // 2
    keeps = jnp.logical_not(gives)
    takes_set = (takes, z == 0)
    gives_set = (gives & (z < zs - 1), z == zs - 1)
    taker = (at(z + zs // 2, y, core), at(z + 1, y, core))

    barrier = pltpu.get_barrier_semaphore()

    def greet(peer):
        pl.semaphore_signal(barrier, inc=1, device_id=peer, device_id_type=MESH)

    def along(place, size, next_peer, first_to_last, act):
        pl.when(place < size - 1)(lambda: act(next_peer))
        pl.when(place == 0)(lambda: act(first_to_last))

    def waited_for(place, size):
        return (place + size - 2) // (size - 1) + place // (size - 1)

    for peer in (right, left, core_peer):
        greet(peer)
    along(y, ys, y_peers[0], y_peers[1], greet)
    along(z, zs, z_peers[0], z_peers[1], greet)
    before = waited_for(y, ys) + waited_for(z, zs)

    block_copies = []
    for block in range(4):
        columns = pl.ds(block * mine, mine)
        block_copies.append(
            pltpu.make_async_copy(scores.at[:, columns], held.at[:, columns], local_sem.at[block])
        )
    student_copy = pltpu.make_async_copy(student_in, student, local_sem.at[4])
    for copy in (student_copy, *block_copies):
        copy.start()
    weights[0] = jnp.full((1, LANES), weight[0], jnp.float32)

    pl.semaphore_wait(barrier, 3 + before)

    def remote(source, target, send, recv, peer):
        return pltpu.make_async_remote_copy(
            src_ref=source,
            dst_ref=target,
            send_sem=send,
            recv_sem=recv,
            device_id=peer,
            device_id_type=MESH,
        )

    far = lax.rem(x + 2, 4)
    two_hop_base = (far * mine + half, far * mine)
    next_base = (lax.rem(x + 1, 4) * mine + half, lax.rem(x + 3, 4) * mine)
    one_hop_base = (lax.rem(x + 1, 4) * mine, lax.rem(x + 3, 4) * mine + half)
    pieces = half // LANES

    weight_copies = [
        remote(weights.at[0], weights.at[1 + side], weight_send.at[side], weight_recv.at[side], sides[side])
        for side in range(2)
    ]
    for copy in weight_copies:
        copy.start()

    class Either:
        def __init__(self, make, first, last):
            self.whole = make(first, last)
            self.less = make(GIVEN, last) if first < GIVEN else None

        def do(self, act):
            if self.less is None:
                act(self.whole)
            else:
                pl.when(keeps)(lambda: act(self.whole))
                pl.when(gives)(lambda: act(self.less))

        def start(self):
            self.do(lambda copy: copy.start())

        def wait_recv(self):
            self.do(lambda copy: copy.wait_recv())

        def wait_send(self):
            self.do(lambda copy: copy.wait_send())

    def raw(kind, bases, buffer, piece, side):
        columns = pl.ds(pl.multiple_of(bases[side] + piece * LANES, LANES), LANES)
        slot = (2 * kind + side) * pieces + piece

        def make(first, last):
            rows = pl.ds(first, last - first)
            return remote(
                scores.at[rows, columns],
                buffer.at[side, rows, pl.ds(piece * LANES, LANES)],
                raw_send.at[slot],
                raw_recv.at[slot],
                sides[side],
            )

        return Either(make, 0, vocab_rows)

    opposite_copies = [[raw(0, two_hop_base, opposite, p, s) for s in range(2)] for p in range(pieces)]
    near_copies = [[raw(1, one_hop_base, near, p, s) for s in range(2)] for p in range(pieces)]
    for pair in opposite_copies:
        for copy in pair:
            copy.start()
    for pair in near_copies[:-1]:
        for copy in pair:
            copy.start()

    def known(stage, peers):
        for peer in peers:
            pl.semaphore_signal(known_sem.at[stage], inc=1, device_id=peer, device_id_type=MESH)

    def answer(place, size, last_peer, last_to_first):
        pl.when(place > 0)(lambda: known(0, (last_peer,)))
        pl.when(place == size - 1)(lambda: known(0, (last_to_first,)))

    answer(y, ys, y_peers[1], y_peers[0])
    answer(z, zs, z_peers[1], z_peers[0])

    wide = 2 * LANES

    def local_stats(ref, first, count, at_column):
        def one(i, _):
            columns = pl.ds(pl.multiple_of(first + i * wide, LANES), wide)

            def peak_body(row, rows, acc):
                whole, rest = folded(ref[pl.ds(row, rows), columns], jnp.maximum, 16)
                acc8, acc4 = acc
                if whole is not None:
                    acc8 = jnp.maximum(acc8, whole)
                if rest is not None:
                    acc4 = jnp.maximum(acc4, rest.astype(jnp.float32).max(axis=0, keepdims=True))
                return acc8, acc4

            low = -1e30
            acc8, acc4 = over_rows(
                0, vocab_rows, peak_body, (jnp.full((16, wide), low, ref.dtype), jnp.full((1, wide), low))
            )
            peak = jnp.maximum(acc8.astype(jnp.float32).max(axis=0, keepdims=True), acc4)

            def total_body(row, rows, acc):
                block = jnp.exp(ref[pl.ds(row, rows), columns].astype(jnp.float32) - peak)
                whole, rest = folded(block, jnp.add)
                acc8, acc4 = acc
                if whole is not None:
                    acc8 = acc8 + whole
                if rest is not None:
                    acc4 = acc4 + rest.sum(axis=0, keepdims=True)
                return acc8, acc4

            acc8, acc4 = over_rows(
                0, vocab_rows, total_body, (jnp.zeros((8, wide)), jnp.zeros((1, wide)))
            )
            put = pl.ds(pl.multiple_of(at_column + i * wide, LANES), wide)
            stats[0:1, put] = peak
            stats[1:2, put] = acc8.sum(axis=0, keepdims=True) + acc4
            return 0

        lax.fori_loop(0, count // wide, one, 0)

    student_copy.wait()
    local_stats(student, 0, mine, tokens)
    pl.when(before < 4)(lambda: pl.semaphore_wait(known_sem.at[0], 4 - before))
    known(1, (*y_peers, *z_peers))
    for block in range(4):
        block_copies[block].wait()
        local_stats(held, block * mine, mine, block * mine)
        if block == 1:
            pl.semaphore_wait(known_sem.at[1], 4)
            known(2, (at(z + 2, y, core), at(z + zs - 2, y, core)))

    def joined(slots):
        peak = stats[0:1]
        for slot in slots:
            peak = jnp.maximum(peak, stats_got[slot, 0:1])
        total = stats[1:2] * jnp.exp(stats[0:1] - peak)
        for slot in slots:
            total = total + stats_got[slot, 1:2] * jnp.exp(stats_got[slot, 0:1] - peak)
        stats[0:1] = peak
        stats[1:2] = total

    def stats_copy(slot, peer, source):
        return remote(source, stats_got.at[slot], stats_send.at[slot], stats_recv.at[slot], peer)

    def round_of(copies):
        for copy in copies:
            copy.start()
        for copy in copies:
            copy.wait()

    round_of([stats_copy(0, core_peer, stats)])
    joined([0])
    round_of([stats_copy(d, at(z, y + d, core), stats) for d in (2, 1, 3)])
    joined([1, 2, 3])
    pl.semaphore_wait(known_sem.at[2], 2)
    round_of([stats_copy(3 + d, at(z + d, y, core), stats) for d in (4, 3, 5, 2, 6, 1, 7)])
    joined(range(4, 11))

    given_rows = pl.ds(0, GIVEN)
    give_copies = [
        [
            remote(source.at[given_rows], target.at[e], give_send.at[2 * e + i], give_recv.at[2 * e + i], taker[e])
            for i, (source, target) in enumerate(((scores, extra), (student_in, extra_student)))
        ]
        for e in range(2)
    ]

    def each_set(predicates, act):
        for e in range(2):
            pl.when(predicates[e])(functools.partial(act, e))

    def start_giving(e):
        for copy in give_copies[e]:
            copy.start()

    each_set(gives_set, start_giving)

    for copy in weight_copies:
        copy.wait()
    relay = remote(weights.at[1], weights.at[3], weight_send.at[2], weight_recv.at[2], right)
    relay.start()
    relay.wait()
    whole_weight = (weights[0] + weights[2]) + (weights[1] + weights[3])
    share = jnp.broadcast_to((weights[0] / whole_weight)[:, 0:1], (1, tokens))

    beside[0, 0:1] = stats[0:1, 0:tokens]
    beside[0, 1:2] = share / stats[1:2, 0:tokens]
    side_copies = [
        remote(beside.at[0], beside.at[1 + side], side_send.at[side], side_recv.at[side], sides[side])
        for side in range(2)
    ]
    for copy in side_copies:
        copy.start()
    for copy in near_copies[-1]:
        copy.start()
    for copy in side_copies:
        copy.wait()

    def term(ref, rows, columns, who, base, width=LANES):
        where = pl.ds(base, width)
        peak, factor = beside[who, 0:1, where], beside[who, 1:2, where]
        return jnp.exp(ref[rows, columns].astype(jnp.float32) - peak) * factor

    cuts = [*CUTS, vocab_rows]

    def sum_copies_of(piece, side):
        columns = pl.ds(piece * LANES, LANES)
        spans = [(0, vocab_rows)] if piece < pieces - 1 else list(zip(cuts[:-1], cuts[1:]))
        result = []
        for i, (first, last) in enumerate(spans):
            slot = (side * pieces + piece) * (len(cuts) - 1) + i

            def make(first, last):
                rows = pl.ds(first, last - first)
                return remote(
                    sent_sum.at[side, rows, columns],
                    got_sum.at[side, rows, columns],
                    sum_send.at[slot],
                    sum_recv.at[slot],
                    sides[side],
                )

            result.append(Either(make, first, last))
        return list(zip(spans, result))

    sum_copies = [[sum_copies_of(p, s) for s in range(2)] for p in range(pieces)]

    extra_part[...] = jnp.zeros_like(extra_part)

    def extra_copy(e, kind, side, source, target):
        slot = 6 * e + 2 * kind + side
        return remote(source, target, extra_send.at[slot], extra_recv.at[slot], sides[side])

    def of_extra(e, bases, side):
        return extra.at[e, :, pl.ds(pl.multiple_of(bases[side], LANES), half)]

    extra_raw = [
        [
            extra_copy(e, kind, side, of_extra(e, bases, side), buffer.at[e, side])
            for kind, (bases, buffer) in enumerate(((two_hop_base, extra_opposite), (one_hop_base, extra_near)))
            for side in range(2)
        ]
        for e in range(2)
    ]
    extra_sums = [
        [extra_copy(e, 2, side, extra_sent.at[e, side], extra_got.at[e, side]) for side in range(2)] for e in range(2)
    ]
    every = pl.ds(0, GIVEN)

    def send_extra_raw(e):
        for copy in give_copies[e]:
            copy.wait_recv()
        for copy in extra_raw[e]:
            copy.start()

    def send_extra_sums(e):
        for side in range(2):
            extra_raw[e][side].wait_recv()
            base = pl.multiple_of(next_base[side], LANES)
            total = term(extra.at[e], every, pl.ds(base, half), 0, base, half) + term(
                extra_opposite.at[e, side], every, pl.ds(0, half), 1 + side, base, half
            )
            extra_sent[e, side] = total.astype(jnp.bfloat16)
            extra_sums[e][side].start()

    def add_extra_pair(e):
        for side in range(2):
            extra_raw[e][2 + side].wait_recv()
            place = side * half
            base = pl.multiple_of(x * mine + place, LANES)
            extra_pair[e, :, place : place + half] = term(extra.at[e], every, pl.ds(base, half), 0, base, half) + term(
                extra_near.at[e, side], every, pl.ds(0, half), 1 + side, base, half
            )

    for piece in range(pieces):
        for side in range(2):
            opposite_copies[piece][side].wait_recv()
        for i, both in enumerate(zip(*sum_copies[piece])):
            for side, ((first, last), copy) in enumerate(both):
                columns = pl.ds(piece * LANES, LANES)
                base = pl.multiple_of(next_base[side] + piece * LANES, LANES)

                def body(row, rows, carry):
                    span = pl.ds(row, rows)
                    total = term(held, span, pl.ds(base, LANES), 0, base) + term(
                        opposite.at[side], span, columns, 1 + side, base
                    )
                    sent_sum[side, span, columns] = total.astype(jnp.bfloat16)
                    return carry

                over_rows(first, last, body, 0)
                copy.start()
            if piece == 0:
                each_set(takes_set, send_extra_raw)
            elif piece == pieces - 1 and i == 0:
                each_set(takes_set, send_extra_sums)

    for piece in range(pieces):
        for side in range(2):
            near_copies[piece][side].wait_recv()
            place = side * half + piece * LANES
            base = pl.multiple_of(x * mine + place, LANES)

            def body(row, rows, carry):
                span = pl.ds(row, rows)
                own_pair[span, pl.ds(place, LANES)] = term(held, span, pl.ds(base, LANES), 0, base) + term(
                    near.at[side], span, pl.ds(piece * LANES, LANES), 1 + side, base
                )
                return carry

            over_rows(0, vocab_rows, body, 0)
    each_set(takes_set, add_extra_pair)

    def hops(d):
        dz, dy = d // plane, d // cores % ys
        return min(dz, zs - dz) + min(dy, ys - dy)

    others = sorted(range(1, zs * plane), key=lambda d: -hops(d))

    def spread(piece):
        for d in others:
            dz, dy, dc = d // plane, d // cores % ys, d % cores
            remote(
                final.at[piece, v],
                final.at[piece, v],
                final_send.at[piece],
                final_recv.at[piece],
                at(z + dz, y + dy, core + dc),
            ).start()

    def spread_done(piece, semaphore):
        every = final.at[piece, pl.ds(0, len(others))]
        pltpu.make_async_copy(every, every, semaphore.at[piece]).wait()

    student_total = jnp.log(stats[1:2, tokens : tokens + mine])

    def divergences(pair, got, logits, place, width):
        mixture = pair + got.astype(jnp.float32)
        student_peak = stats[0:1, tokens + place : tokens + place + width]
        logq = logits.astype(jnp.float32) - student_peak - student_total[:, place : place + width]
        return mixture * (jnp.log(jnp.maximum(mixture, 1e-30)) - logq)

    def divergence_part(piece, side, first, last, acc):
        place = (1 - side) * half + piece * LANES
        here = pl.ds(place, LANES)

        def body(row, rows, acc):
            span = pl.ds(row, rows)
            got = got_sum[side, span, pl.ds(piece * LANES, LANES)]
            value = divergences(own_pair[span, here], got, student[span, here], place, LANES)
            whole, rest = folded(value, jnp.add)
            acc8, acc4 = acc
            if whole is not None:
                acc8 = acc8 + whole
            if rest is not None:
                acc4 = acc4 + rest.sum(axis=0, keepdims=True)
            return acc8, acc4

        return over_rows(first, last, body, acc)

    def add_extra_divergence(e):
        for side in range(2):
            extra_sums[e][side].wait_recv()
            place = (1 - side) * half
            here = pl.ds(place, half)
            value = divergences(extra_pair[e, :, here], extra_got[e, side], extra_student[e, :, here], place, half)
            extra_part[:, here] = extra_part[:, here] + value.sum(axis=0, keepdims=True)

    def add_extra_part(piece, side):
        lanes = pl.ds((1 - side) * LANES, LANES)
        place = (1 - side) * half + piece * LANES
        final[piece, v, :, lanes] = final[piece, v, :, lanes] + extra_part[:, place : place + LANES]

    for piece in range(pieces):
        accs = [(jnp.zeros((8, LANES)), jnp.zeros((1, LANES)))] * 2
        for i, both in enumerate(zip(*sum_copies[piece])):
            for side, ((first, last), copy) in enumerate(both):
                copy.wait_recv()
                if first == 0:
                    head, rest = divergence_part(piece, side, 0, GIVEN, accs[side])
                    accs[side] = jnp.where(gives, 0.0, head), rest
                    first = GIVEN
                accs[side] = divergence_part(piece, side, first, last, accs[side])
            if piece == pieces - 1 and i == 1:

                each_set(takes_set, add_extra_divergence)

                @pl.when(takes)
                def _():
                    for side in range(2):
                        add_extra_part(0, side)
                    spread(0)

        for side in range(2):
            part = accs[side][0].sum(axis=0, keepdims=True) + accs[side][1]
            final[piece, v, :, (1 - side) * LANES : (2 - side) * LANES] = part
            if piece > 0:
                add_extra_part(piece, side)
        if piece == 0:
            pl.when(jnp.logical_not(takes))(functools.partial(spread, 0))
    spread(pieces - 1)
    for piece in range(pieces):
        spread_done(piece, final_recv)
        total = final[piece].sum(axis=0)
        for part in range(2):
            place = part * half + piece * LANES
            out_ref[:, place : place + LANES] = total[:, part * LANES : (part + 1) * LANES]

    for piece in range(pieces):
        spread_done(piece, final_send)
    for piece in range(pieces):
        for side in range(2):
            opposite_copies[piece][side].wait_send()
            near_copies[piece][side].wait_send()
            for _, copy in sum_copies[piece][side]:
                copy.wait_send()

    def extra_sent_out(e):
        for copy in (*extra_raw[e], *extra_sums[e]):
            copy.wait_send()

    def given(e):
        for copy in give_copies[e]:
            copy.wait_send()

    each_set(takes_set, extra_sent_out)
    each_set(gives_set, given)


def solution(mesh):
    def local(teacher_logits, teacher_weight, student_logits):
        scores, student = teacher_logits[0].T, student_logits.T
        vocab_rows, tokens = scores.shape
        mine = student.shape[1]
        half = mine // 2
        pieces = half // LANES
        ys, cores = 4, 2
        everyone = mesh.shape["vocab"]
        zs = everyone // (ys * cores)
        together = tokens + mine
        f32, bf16 = jnp.float32, jnp.bfloat16
        dma = pltpu.SemaphoreType.DMA
        out = pl.pallas_call(
            functools.partial(kernel, (vocab_rows, tokens, mine, cores, ys, zs)),
            out_shape=pltpu.VMEM((1, mine), f32),
            in_specs=[
                pl.BlockSpec(memory_space=pltpu.SMEM),
                pl.BlockSpec(memory_space=pltpu.HBM),
                pl.BlockSpec(memory_space=pltpu.HBM),
            ],
            out_specs=pl.BlockSpec(memory_space=pltpu.VMEM),
            scratch_shapes=[
                pltpu.VMEM((vocab_rows, tokens), bf16),
                pltpu.VMEM((vocab_rows, mine), bf16),
                pltpu.VMEM((2, vocab_rows, half), bf16),
                pltpu.VMEM((2, vocab_rows, half), bf16),
                pltpu.VMEM((2, vocab_rows, half), bf16),
                pltpu.VMEM((2, vocab_rows, half), bf16),
                pltpu.VMEM((vocab_rows, mine), f32),
                pltpu.VMEM((2, together), f32),
                pltpu.VMEM((11, 2, together), f32),
                pltpu.VMEM((3, 2, tokens), f32),
                pltpu.VMEM((4, 1, LANES), f32),
                pltpu.VMEM((pieces, everyone, 1, 2 * LANES), f32),
                pltpu.VMEM((2, GIVEN, tokens), bf16),
                pltpu.VMEM((2, GIVEN, mine), bf16),
                pltpu.VMEM((2, 2, GIVEN, half), bf16),
                pltpu.VMEM((2, 2, GIVEN, half), bf16),
                pltpu.VMEM((2, 2, GIVEN, half), bf16),
                pltpu.VMEM((2, 2, GIVEN, half), bf16),
                pltpu.VMEM((2, GIVEN, mine), f32),
                pltpu.VMEM((1, mine), f32),
                dma((5,)),
                dma((4 * pieces,)),
                dma((4 * pieces,)),
                dma((2 * pieces * len(CUTS),)),
                dma((2 * pieces * len(CUTS),)),
                dma((11,)),
                dma((11,)),
                dma((2,)),
                dma((2,)),
                dma((3,)),
                dma((3,)),
                dma((pieces,)),
                dma((pieces,)),
                pltpu.SemaphoreType.REGULAR((3,)),
                dma((4,)),
                dma((4,)),
                dma((12,)),
                dma((12,)),
            ],
            compiler_params=pltpu.CompilerParams(
                collective_id=0, has_side_effects=True, vmem_limit_bytes=60 * 1024 * 1024
            ),
        )(teacher_weight, *(pltpu.with_memory_space_constraint(a, pltpu.HBM) for a in (scores, student)))
        return out.reshape(mine)

    in_specs = (P("teach", "tok", "vocab"), P("teach"), P(("tok", "teach"), "vocab"))
    out_specs = P(("tok", "teach"))
    return jax.shard_map(local, mesh=mesh, in_specs=in_specs, out_specs=out_specs, check_vma=False)
```
